32 devices in a mesh: groups: 2 (over y), shard: 16 (over z, x, core).
Axes of the slice: x: 2, y: 2, z: 4, core: 2. Of those that a mesh axis runs over, the one named last changes fastest.
Arguments:
- query_tokens: bfloat16 [1024, 32, 128], P(('groups', 'shard')), parts along dimension 0, may hold values from -0.1875 to 0.1875
- candidates: int32 [1024, 24], P(('groups', 'shard')), parts along dimension 0, may hold values from 0 to 511, as said below
- cand_count: int32 [1024], P(('groups', 'shard')), parts along dimension 0, may hold values from 3 to 24, as said below
- placement_map: int32 [1024], P('groups'), parts along dimension 0, may hold values from 0 to 511, as said below
- passage_base: bfloat16 [1024, 128, 128], P(('groups', 'shard')), parts along dimension 0, may hold values from -6 to 6
- residual_codes: int32 [1024, 128, 128], P(('groups', 'shard')), parts along dimension 0, may hold values from 0 to 3
- passage_lengths: int32 [1024], P(('groups', 'shard')), parts along dimension 0, may hold values from 32 to 128
- bucket_weights: float32 [8], P('groups'), parts along dimension 0, may hold values from -3 to 3
Outputs:
- scores: float32 [1024, 24], P(('groups', 'shard')), parts along dimension 0
The draws below stay inside these ranges and needn't reach their ends.
There are 2 independent parts, one for each index of `groups`. The reference program is written for one: setup_inputs(seed, part) draws one part's arguments, and reference() takes and returns one part's arrays. A program takes and returns all parts, laid end to end along the dimension named above; each array names one. Nothing has to cross between parts.
Inputs may be any that keep to these rules, and one draw needn't show every extreme that they name: In row q the first cand_count[q] entries are distinct passage ids; the devices that store them (device placement_map[id] // 32 of the shard axis) are at most 3, and one device stores at most 8 of them. Of the 32 queries of one device, one storing device (the same for all devices) holds candidates of exactly 9, and every other storing device holds candidates of at most 6. Entries at or beyond cand_count[q] are arbitrary ids. `cand_count`: entries of candidates at or beyond this count are not scored. A permutation: passage id p is row placement_map[p] of the passage store.
All inputs are finite; a program needn't handle non-finite values.
Results may differ from the reference program's by a relative error of at most 0.0003.
Values may be sent and summed in bfloat16 or wider, within the bound.
A program may use at most 64 MiB of HBM per device.

```python
import jax
import jax.numpy as jnp
from jax import lax

DIM = 128
QLEN = 32
PLEN = 128
OWNERS_Q = 3
CPQ = 8
Q_DEV = 32
P_DEV = 32
NQ = 512
P_TOTAL = 512
CMAX = 24
HOTQ = 9
N_SHARD = 16


def layout(key):
    device_count = N_SHARD
    folded = jax.random.fold_in(key, 911)
    streams = jax.random.split(folded, 8)
    placed = jax.random.permutation(streams[0], P_TOTAL).astype(jnp.int32)
    inverse = jnp.argsort(placed).astype(jnp.int32)
    hottest = jax.random.randint(streams[1], (), 0, device_count, dtype=jnp.int32)
    others = jax.random.permutation(streams[2], device_count - 1).astype(jnp.int32)
    others = others + (others >= hottest).astype(jnp.int32)
    offset = jax.random.randint(streams[3], (device_count, 1, 1), 0, Q_DEV, dtype=jnp.int32)
    query_idx = jnp.arange(Q_DEV, dtype=jnp.int32)[None, :, None]
    owner_idx = jnp.arange(OWNERS_Q, dtype=jnp.int32)[None, None, :]
    turned = (query_idx - offset) % Q_DEV
    is_hot = (owner_idx == 0) & (turned < HOTQ)
    prior_offset = jnp.minimum(turned + (owner_idx > 0).astype(jnp.int32), HOTQ)
    position = turned * OWNERS_Q + owner_idx - prior_offset
    holders = jnp.where(is_hot, hottest, others[position % (device_count - 1)])
    filled = is_hot | (turned == 0)
    shape3 = (device_count, Q_DEV, OWNERS_Q)
    counts = jnp.where(filled, CPQ, jax.random.randint(streams[4], shape3, 1, CPQ + 1, dtype=jnp.int32))
    ranking = jax.random.randint(streams[5], shape3 + (P_DEV,), 0, 4096, dtype=jnp.int32) * P_DEV + jnp.arange(P_DEV, dtype=jnp.int32)
    picked_rows = jnp.argsort(ranking, axis=-1)[..., :CPQ].astype(jnp.int32)
    chosen = inverse[holders[..., None] * P_DEV + picked_rows]
    usable = jnp.arange(CPQ, dtype=jnp.int32) < counts[..., None]
    filler = jax.random.randint(streams[6], shape3 + (CPQ,), 0, P_TOTAL, dtype=jnp.int32)
    chosen = jnp.where(usable, chosen, filler).reshape(device_count, Q_DEV, CMAX)
    usable = usable.reshape(device_count, Q_DEV, CMAX)
    mixing = jax.random.randint(streams[7], (device_count, Q_DEV, CMAX), 0, 4096, dtype=jnp.int32) * CMAX + jnp.arange(CMAX, dtype=jnp.int32)
    sort_key = jnp.where(usable, 0, 4096 * CMAX) + mixing
    picked = jnp.argsort(sort_key, axis=-1)
    chosen = jnp.take_along_axis(chosen, picked, axis=-1)
    totals = jnp.sum(counts, axis=-1).astype(jnp.int32)
    return (placed, chosen.reshape(NQ, CMAX), totals.reshape(NQ))


def draw_candidates(key, part):
    return layout(key)[1]


def draw_cand_count(key, part):
    return layout(key)[2]


def draw_placement_map(key, part):
    return layout(key)[0]


def touch_ends(array, key, smallest, largest):
    spot = [jax.random.randint(jax.random.fold_in(key, axis), (), 0, length) for axis, length in enumerate(array.shape)]
    longest = array.shape.index(max(array.shape))
    neighbour = spot[:longest] + [(spot[longest] + 1) % array.shape[longest]] + spot[longest + 1:]
    return array.at[tuple(spot)].set(smallest).at[tuple(neighbour)].set(largest)


def level_of(stream_key, dims, shards, least, largest):
    loudness, own = 1.0, jax.random.fold_in(stream_key, 6)
    for dim, shards_of in shards:
        heights = jnp.exp(jax.random.uniform(jax.random.fold_in(own, dim), (shards_of,), jnp.float32, least / len(shards), largest / len(shards)))
        loudness = loudness * jnp.repeat(heights, dims[dim] // shards_of).reshape([-1 if axis == dim else 1 for axis in range(len(dims))])
    return loudness


def bell_draw(stream_key, dims, scale, bound, shards=(), held_as=jnp.bfloat16):
    factor_of = level_of(stream_key, dims, shards, -0.22, 0.18) if shards else 1.0
    entries = jax.random.normal(stream_key, dims, jnp.float32) * scale * factor_of
    return jnp.minimum(jnp.maximum(entries, -bound), bound).astype(held_as)


def setup_inputs(seed: int = 0, part: int = 0) -> dict:
    splits = jax.random.split(jax.random.key(seed), 9)
    part_keys = jax.random.split(jax.random.fold_in(splits[8], part), 9)
    return {
        "query_tokens": bell_draw(part_keys[0], (NQ, QLEN, DIM), (1.0 / QLEN), 0.1875, ((0, 16),)),
        "candidates": draw_candidates(jax.random.fold_in(jax.random.fold_in(splits[8], part), 71), part),
        "cand_count": draw_cand_count(jax.random.fold_in(jax.random.fold_in(splits[8], part), 71), part),
        "placement_map": draw_placement_map(jax.random.fold_in(jax.random.fold_in(splits[8], part), 71), part),
        "passage_base": bell_draw(part_keys[4], (P_TOTAL, PLEN, DIM), 1.0, 6.0, ((0, 16),)),
        "residual_codes": touch_ends(jax.random.randint(part_keys[5], (P_TOTAL, PLEN, DIM), 0, 4), jax.random.fold_in(part_keys[5], 1), 0, 3).astype(jnp.int32),
        "passage_lengths": touch_ends(jax.random.randint(part_keys[6], (P_TOTAL,), PLEN // 4, PLEN + 1), jax.random.fold_in(part_keys[6], 1), PLEN // 4, PLEN).astype(jnp.int32),
        "bucket_weights": bell_draw(part_keys[7], (4,), 0.5, 3.0, (), jnp.float32),
    }


epsilon = 1e-06
negative = -1e+30

def decode(bases, code_ids, levels):
    residual = jnp.zeros(bases.shape, jnp.float32)
    for bucket in range(4):
        residual = residual + jnp.where(code_ids == bucket, levels[bucket], 0.0)
    summed = bases.astype(jnp.float32) + residual
    inverse_norm = lax.rsqrt(lax.optimization_barrier(jnp.sum(summed * summed, axis=-1, keepdims=True)) + epsilon)
    return (summed * inverse_norm).astype(jnp.bfloat16)

def reference(query_tokens, candidates, cand_count, placement_map, passage_base, residual_codes, passage_lengths, bucket_weights):

    def decode_block(bundle):
        return decode(bundle[0], bundle[1], bucket_weights)
    decoded = lax.map(decode_block, (passage_base.reshape(N_SHARD, P_DEV, PLEN, DIM), residual_codes.reshape(N_SHARD, P_DEV, PLEN, DIM)))
    decoded = decoded.reshape(P_TOTAL, PLEN, DIM)

    def score_block(bundle):
        query_rows, listed, counted = bundle
        stored = placement_map[listed]
        token_rows = decoded[stored].astype(jnp.float32)
        lengths = passage_lengths[stored]
        similarity_scores = jnp.einsum('tug,terg->tuer', query_rows.astype(jnp.float32), token_rows)
        inside = jnp.arange(PLEN, dtype=jnp.int32)[None, None, None, :] < lengths[:, None, :, None]
        maxima = lax.optimization_barrier(jnp.max(jnp.where(inside, similarity_scores, negative), axis=3))
        summed = lax.optimization_barrier(jnp.sum(maxima, axis=1))
        usable = jnp.arange(CMAX, dtype=jnp.int32)[None, :] < counted[:, None]
        return jnp.where(usable, summed, 0.0)
    scored = lax.map(score_block, (query_tokens.reshape(N_SHARD, Q_DEV, QLEN, DIM), candidates.reshape(N_SHARD, Q_DEV, CMAX), cand_count.reshape(N_SHARD, Q_DEV)))
    return scored.reshape(NQ, CMAX)
```

```python
import functools

import jax
import jax.numpy as jnp
from jax import lax
from jax.experimental import pallas as pl
from jax.experimental.pallas import tpu as pltpu
from jax.sharding import PartitionSpec as P

OWNERS_Q = 3
CHUNK = 8
LANES = 128
EPSILON = 1e-06
AXIS = "shard"

NT = (((1,), (1,)), ((), ()))
NN = (((1,), (0,)), ((), ()))


def dot(a, b, dims):
    return lax.dot_general(a, b, dims, preferred_element_type=jnp.float32)


def split_dot(a, b, dims, exact_left):
    full = b if exact_left else a
    high = full.astype(jnp.bfloat16)
    low = (full - high.astype(jnp.float32)).astype(jnp.bfloat16)
    if exact_left:
        return dot(a, high, dims) + dot(a, low, dims)
    return dot(high, b, dims) + dot(low, b, dims)


def iota(shape, axis):
    return lax.broadcasted_iota(jnp.int32, shape, axis)


def kernel(
    n,
    cap,
    weights_ref,
    lengths_ref,
    queries_ref,
    candidates_ref,
    count_ref,
    placement_ref,
    base_hbm,
    codes_hbm,
    out_ref,
    base_ref,
    codes_ref,
    tokens_ref,
    send_ref,
    recv_ref,
    source_vmem,
    source_smem,
    maxima_ref,
    scores_ref,
    returned_ref,
    load_sem,
    source_sem,
    send_sem,
    recv_sem,
    back_send_sem,
    back_recv_sem,
):
    me = lax.axis_index(AXIS)
    rows, plen, dim = base_ref.shape
    count, qlen, _ = queries_ref.shape
    slots = candidates_ref.shape[1]
    total = placement_ref.shape[1]
    padded = scores_ref.shape[1]
    per_group = LANES // rows
    groups = n // per_group
    steps = n * cap // CHUNK

    def partner(offset):
        return lax.rem(me + offset, n)

    def holder_of_mine(offset):
        return lax.rem(me + n - offset, n)

    load_base = pltpu.make_async_copy(base_hbm, base_ref, load_sem.at[0])
    load_codes = pltpu.make_async_copy(codes_hbm, codes_ref, load_sem.at[1])
    load_base.start()
    load_codes.start()

    barrier = pltpu.get_barrier_semaphore()

    def greet(offset, carry):
        pl.semaphore_signal(barrier, inc=1, device_id={AXIS: partner(offset)}, device_id_type=pl.DeviceIdType.MESH)
        return carry

    lax.fori_loop(1, n, greet, 0)

    candidates = candidates_ref[...]
    counted = count_ref[...]
    placement = placement_ref[...].astype(jnp.float32)
    passage_iota = iota((count, total), 1)
    slot_iota = iota((count, slots), 1)
    holder_iota = iota((count, LANES), 1)
    stored_cols = []
    present = jnp.zeros((count, LANES), jnp.float32)
    for c in range(slots):
        hit = passage_iota == candidates[:, c : c + 1]
        found = jnp.sum(jnp.where(hit, placement, 0.0), axis=1, keepdims=True).astype(jnp.int32)
        stored_cols.append(found)
        holder = jnp.where(c < counted, found // rows, -1)
        present = jnp.where(holder_iota == holder, 1.0, present)
    earlier = (iota((count, count), 1) < iota((count, count), 0)).astype(jnp.bfloat16)
    slot_of = dot(earlier, present.astype(jnp.bfloat16), NN)
    slot_of = jnp.where(present > 0.0, slot_of, -1.0).astype(jnp.bfloat16)
    eye = (iota((n, LANES), 0) == iota((n, LANES), 1)).astype(jnp.bfloat16)
    slot_by_holder = dot(eye, slot_of, NT)
    query_iota = iota((n, count), 1)
    lane_iota = iota((n, LANES), 1)
    source = jnp.zeros((n, LANES), jnp.int32)
    for s in range(cap):
        which = jnp.sum(
            jnp.where(slot_by_holder == float(s), query_iota.astype(jnp.float32), 0.0), axis=1, keepdims=True
        ).astype(jnp.int32)
        source = jnp.where(lane_iota == s, which, source)
    source_vmem[...] = source

    maxima_ref[...] = jnp.zeros_like(maxima_ref)
    scores_ref[...] = jnp.zeros_like(scores_ref)

    to_scalar = pltpu.make_async_copy(source_vmem, source_smem, source_sem)
    to_scalar.start()
    to_scalar.wait()

    def query_for(holder, s):
        return queries_ref[jnp.minimum(jnp.maximum(source_smem[holder, s], 0), count - 1)]

    def pack(offset, carry):
        holder = partner(offset)
        for s in range(cap):
            send_ref[offset, s] = query_for(holder, s)
        return carry

    def outgoing(offset):
        return pltpu.make_async_remote_copy(
            src_ref=send_ref.at[offset],
            dst_ref=recv_ref.at[offset],
            send_sem=send_sem.at[offset],
            recv_sem=recv_sem.at[offset],
            device_id={AXIS: partner(offset)},
            device_id_type=pl.DeviceIdType.MESH,
        )

    pack(1, 0)
    pl.semaphore_wait(barrier, n - 1)

    def pack_and_send(offset, carry):
        pack(offset + 1, 0)
        outgoing(offset).start()
        return carry

    lax.fori_loop(1, n - 1, pack_and_send, 0)
    for s in range(cap):
        recv_ref[0, s] = query_for(me, s)
    outgoing(n - 1).start()

    load_base.wait()
    load_codes.wait()
    token_iota = iota((plen, dim), 0)

    def decode(r, carry):
        codes = codes_ref[r]
        low = jnp.where(codes < 1, weights_ref[0, 0], weights_ref[0, 1])
        high = jnp.where(codes < 3, weights_ref[0, 2], weights_ref[0, 3])
        summed = base_ref[r].astype(jnp.float32) + jnp.where(codes < 2, low, high)
        inverse = lax.rsqrt(jnp.sum(summed * summed, axis=1, keepdims=True) + EPSILON)
        unit = summed * inverse
        unit = jnp.where(token_iota < lengths_ref[0, r], unit, unit[0:1, :])
        tokens_ref[r] = unit.astype(jnp.bfloat16)
        return carry

    lax.fori_loop(0, rows, decode, 0)

    row_start = lax.rem(me, per_group) * rows
    gather_tokens = (iota((CHUNK, CHUNK * qlen), 1) // qlen == iota((CHUNK, CHUNK * qlen), 0)).astype(jnp.bfloat16)

    def back(offset):
        return pltpu.make_async_remote_copy(
            src_ref=scores_ref.at[offset],
            dst_ref=returned_ref.at[me],
            send_sem=back_send_sem.at[offset],
            recv_sem=back_recv_sem.at[me],
            device_id={AXIS: holder_of_mine(offset)},
            device_id_type=pl.DeviceIdType.MESH,
        )

    def send_back(offset, carry):
        back(offset).start()
        return carry

    def chunk(i, carry):
        first, last = i * CHUNK, i * CHUNK + CHUNK - 1
        lax.fori_loop((first - 1 + cap) // cap, last // cap + 1, wait_query_if, 0)
        parts = [recv_ref[(first + g) // cap, lax.rem(first + g, cap)] for g in range(CHUNK)]
        block = jnp.concatenate(parts, axis=0)

        def one_row(r, inner):
            similar = dot(tokens_ref[r], block, NT)
            maxima_ref[pl.ds(row_start + r, 1), :] = jnp.max(similar, axis=0, keepdims=True)
            return inner

        lax.fori_loop(0, rows, one_row, 0, unroll=4)
        scored = split_dot(gather_tokens, maxima_ref[...], NT, True)
        for g in range(CHUNK):
            scores_ref[(first + g) // cap, pl.ds(lax.rem(first + g, cap), 1), :] = scored[g : g + 1, :]
        lax.fori_loop(jnp.maximum(done_before(i - 1), 1), jnp.maximum(done_before(i), 1), send_back, 0)
        return carry

    def done_before(i):
        return jnp.maximum(i, 0) * CHUNK // cap

    def wait_query_if(offset, carry):
        @pl.when(offset >= 1)
        def _():
            outgoing(offset).wait_recv()

        return carry

    lax.fori_loop(0, steps, chunk, 0)

    def wait_sent(offset, carry):
        outgoing(offset).wait_send()
        return carry

    lax.fori_loop(1, n, wait_sent, 0)
    lax.fori_loop(max((steps - 1) * CHUNK // cap, 1), n, send_back, 0)
    returned_ref[me] = scores_ref[0]

    spread = (iota((LANES, n * padded), 1) // padded == iota((LANES, n * padded), 0)).astype(jnp.bfloat16)
    wide_slot = dot(slot_of, spread, NN)
    wide_iota = iota((count, n * padded), 1)
    chosen = wide_slot == lax.rem(wide_iota, padded).astype(jnp.float32)
    picks = jnp.concatenate(
        [
            jnp.where(chosen & (wide_iota // (padded * per_group) == g), 1.0, 0.0).astype(jnp.bfloat16)
            for g in range(groups)
        ],
        axis=0,
    )

    def wait_back(offset, carry):
        peer = partner(offset)
        pltpu.make_async_remote_copy(
            src_ref=scores_ref.at[offset],
            dst_ref=returned_ref.at[peer],
            send_sem=back_send_sem.at[offset],
            recv_sem=back_recv_sem.at[peer],
            device_id={AXIS: peer},
            device_id_type=pl.DeviceIdType.MESH,
        ).wait_recv()
        return carry

    lax.fori_loop(1, n, wait_back, 0)
    values = split_dot(picks, returned_ref[...].reshape(n * padded, LANES), NN, True)
    result = jnp.zeros((count, slots), jnp.float32)
    for c in range(slots):
        kept = jnp.zeros((count, LANES), jnp.float32)
        for g in range(groups):
            kept = jnp.where(
                holder_iota + g * LANES == stored_cols[c], values[g * count : (g + 1) * count, :], kept
            )
        result = jnp.where(slot_iota == c, jnp.sum(kept, axis=1, keepdims=True), result)
    out_ref[...] = jnp.where(slot_iota < counted, result, 0.0)

    def wait_back_sent(offset, carry):
        back(offset).wait_send()
        return carry

    lax.fori_loop(1, n, wait_back_sent, 0)


def local(
    query_tokens,
    candidates,
    cand_count,
    placement_map,
    passage_base,
    residual_codes,
    passage_lengths,
    bucket_weights,
):
    n = lax.axis_size(AXIS)
    count, qlen, dim = query_tokens.shape
    slots = candidates.shape[1]
    rows, plen, _ = passage_base.shape
    cap = count * OWNERS_Q // n + 3
    padded = -(-cap // 8) * 8
    vmem = pl.BlockSpec(memory_space=pltpu.VMEM)
    smem = pl.BlockSpec(memory_space=pltpu.SMEM)
    anywhere = pl.BlockSpec(memory_space=pl.ANY)
    return pl.pallas_call(
        functools.partial(kernel, n, cap),
        out_shape=jax.ShapeDtypeStruct((count, slots), jnp.float32),
        in_specs=[smem, smem, vmem, vmem, vmem, vmem, anywhere, anywhere],
        out_specs=vmem,
        scratch_shapes=[
            pltpu.VMEM((rows, plen, dim), passage_base.dtype),
            pltpu.VMEM((rows, plen, dim), jnp.int32),
            pltpu.VMEM((rows, plen, dim), jnp.bfloat16),
            pltpu.VMEM((n, cap, qlen, dim), jnp.bfloat16),
            pltpu.VMEM((n, cap, qlen, dim), jnp.bfloat16),
            pltpu.VMEM((n, LANES), jnp.int32),
            pltpu.SMEM((n, LANES), jnp.int32),
            pltpu.VMEM((LANES, CHUNK * qlen), jnp.float32),
            pltpu.VMEM((n, padded, LANES), jnp.float32),
            pltpu.VMEM((n, padded, LANES), jnp.float32),
            pltpu.SemaphoreType.DMA((2,)),
            pltpu.SemaphoreType.DMA,
            pltpu.SemaphoreType.DMA((n,)),
            pltpu.SemaphoreType.DMA((n,)),
            pltpu.SemaphoreType.DMA((n,)),
            pltpu.SemaphoreType.DMA((n,)),
        ],
        compiler_params=pltpu.CompilerParams(
            collective_id=0, has_side_effects=True, vmem_limit_bytes=48 * 1024 * 1024
        ),
        name="rerank",
    )(
        bucket_weights.reshape(1, -1),
        passage_lengths.reshape(1, -1),
        query_tokens,
        candidates,
        cand_count.reshape(-1, 1),
        placement_map.reshape(1, -1),
        passage_base,
        residual_codes,
    )


def solution(mesh):
    split = P(("groups", "shard"))
    return jax.shard_map(
        local,
        mesh=mesh,
        in_specs=(
            P(("groups", "shard"), None, None),
            P(("groups", "shard"), None),
            split,
            P("groups"),
            P(("groups", "shard"), None, None),
            P(("groups", "shard"), None, None),
            split,
            P("groups"),
        ),
        out_specs=P(("groups", "shard"), None),
        check_vma=False,
    )
```

```python
import functools

import jax
import jax.numpy as jnp
from jax import lax
from jax.experimental import pallas as pl
from jax.experimental.pallas import tpu as pltpu
from jax.sharding import PartitionSpec as P

OWNERS_Q = 3
CHUNK = 8
LANES = 128
EPSILON = 1e-06
AXIS = "shard"

NT = (((1,), (1,)), ((), ()))
NN = (((1,), (0,)), ((), ()))


def dot(a, b, dims):
    return lax.dot_general(a, b, dims, preferred_element_type=jnp.float32)


def split_dot(a, b, dims, exact_left):
    full = b if exact_left else a
    high = full.astype(jnp.bfloat16)
    low = (full - high.astype(jnp.float32)).astype(jnp.bfloat16)
    if exact_left:
        return dot(a, high, dims) + dot(a, low, dims)
    return dot(high, b, dims) + dot(low, b, dims)


def iota(shape, axis):
    return lax.broadcasted_iota(jnp.int32, shape, axis)


def kernel(
    n,
    cap,
    weights_hbm,
    lengths_hbm,
    queries_hbm,
    candidates_hbm,
    count_hbm,
    placement_hbm,
    base_hbm,
    codes_hbm,
    out_ref,
    weights_ref,
    lengths_ref,
    queries_ref,
    candidates_ref,
    count_ref,
    placement_ref,
    base_ref,
    codes_ref,
    tokens_ref,
    send_ref,
    recv_ref,
    source_vmem,
    source_smem,
    maxima_ref,
    scores_ref,
    returned_ref,
    load_sem,
    source_sem,
    send_sem,
    recv_sem,
    back_send_sem,
    back_recv_sem,
):
    me = lax.axis_index(AXIS)
    rows, plen, dim = base_ref.shape
    count, qlen, _ = queries_ref.shape
    slots = candidates_ref.shape[0]
    total = placement_ref.shape[1]
    padded = scores_ref.shape[1]
    per_group = LANES // rows
    groups = n // per_group
    steps = n * cap // CHUNK

    def partner(offset):
        return lax.rem(me + offset, n)

    def holder_of_mine(offset):
        return lax.rem(me + n - offset, n)

    pairs = (
        (candidates_hbm, candidates_ref),
        (count_hbm, count_ref),
        (placement_hbm, placement_ref),
        (queries_hbm, queries_ref),
        (weights_hbm, weights_ref),
        (lengths_hbm, lengths_ref),
        (base_hbm, base_ref),
        (codes_hbm, codes_ref),
    )
    loads = [pltpu.make_async_copy(src, dst, load_sem.at[i]) for i, (src, dst) in enumerate(pairs)]
    for load in loads:
        load.start()

    barrier = pltpu.get_barrier_semaphore()

    def greet(offset, carry):
        pl.semaphore_signal(barrier, inc=1, device_id={AXIS: partner(offset)}, device_id_type=pl.DeviceIdType.MESH)
        return carry

    lax.fori_loop(1, n, greet, 0)

    for load in loads[:3]:
        load.wait()
    square = (iota((count, count), 0) == iota((count, count), 1)).astype(jnp.bfloat16)

    def upright(flat):
        return dot(square, flat.astype(jnp.float32).astype(jnp.bfloat16), NT).astype(jnp.int32)

    listed = candidates_ref[...]
    candidates = upright(lax.div(listed, 64)) * 64 + upright(lax.rem(listed, 64))
    counted = upright(jnp.broadcast_to(count_ref[...], (8, count)))[:, 0:1]
    placement = placement_ref[...].astype(jnp.float32)
    passage_iota = iota((count, total), 1)
    slot_iota = iota((count, slots), 1)
    holder_iota = iota((count, LANES), 1)
    stored_cols = []
    present = jnp.zeros((count, LANES), jnp.float32)
    for c in range(slots):
        hit = passage_iota == candidates[:, c : c + 1]
        found = jnp.sum(jnp.where(hit, placement, 0.0), axis=1, keepdims=True).astype(jnp.int32)
        stored_cols.append(found)
        holder = jnp.where(c < counted, lax.div(found, rows), -1)
        present = jnp.where(holder_iota == holder, 1.0, present)
    earlier = (iota((count, count), 1) < iota((count, count), 0)).astype(jnp.bfloat16)
    slot_of = dot(earlier, present.astype(jnp.bfloat16), NN)
    slot_of = jnp.where(present > 0.0, slot_of, -1.0).astype(jnp.bfloat16)
    eye = (iota((n, LANES), 0) == iota((n, LANES), 1)).astype(jnp.bfloat16)
    slot_by_holder = dot(eye, slot_of, NT)
    query_iota = iota((n, count), 1)
    lane_iota = iota((n, LANES), 1)
    source = jnp.zeros((n, LANES), jnp.int32)
    for s in range(cap):
        which = jnp.sum(
            jnp.where(slot_by_holder == float(s), query_iota.astype(jnp.float32), 0.0), axis=1, keepdims=True
        ).astype(jnp.int32)
        source = jnp.where(lane_iota == s, which, source)
    source_vmem[...] = source

    maxima_ref[...] = jnp.zeros_like(maxima_ref)
    scores_ref[...] = jnp.zeros_like(scores_ref)

    to_scalar = pltpu.make_async_copy(source_vmem, source_smem, source_sem)
    to_scalar.start()
    loads[3].wait()
    to_scalar.wait()

    def query_for(holder, s):
        return queries_ref[jnp.minimum(jnp.maximum(source_smem[holder, s], 0), count - 1)]

    def pack(offset, carry):
        holder = partner(offset)
        for s in range(cap):
            send_ref[offset * cap + s] = query_for(holder, s)
        return carry

    def outgoing(offset):
        return pltpu.make_async_remote_copy(
            src_ref=send_ref.at[pl.ds(offset * cap, cap)],
            dst_ref=recv_ref.at[pl.ds(offset * cap, cap)],
            send_sem=send_sem.at[offset],
            recv_sem=recv_sem.at[offset],
            device_id={AXIS: partner(offset)},
            device_id_type=pl.DeviceIdType.MESH,
        )

    pack(1, 0)
    pl.semaphore_wait(barrier, n - 1)

    def pack_and_send(offset, carry):
        pack(offset + 1, 0)
        outgoing(offset).start()
        return carry

    lax.fori_loop(1, n - 1, pack_and_send, 0)
    for s in range(cap):
        recv_ref[s] = query_for(me, s)
    outgoing(n - 1).start()

    for load in loads[4:]:
        load.wait()
    token_iota = iota((plen, dim), 0)

    def decode(r, carry):
        codes = codes_ref[r]
        low = jnp.where(codes < 1, weights_ref[0, 0], weights_ref[0, 1])
        high = jnp.where(codes < 3, weights_ref[0, 2], weights_ref[0, 3])
        summed = base_ref[r].astype(jnp.float32) + jnp.where(codes < 2, low, high)
        inverse = lax.rsqrt(jnp.sum(summed * summed, axis=1, keepdims=True) + EPSILON)
        unit = summed * inverse
        unit = jnp.where(token_iota < lengths_ref[0, r], unit, unit[0:1, :])
        tokens_ref[r] = unit.astype(jnp.bfloat16)
        return carry

    lax.fori_loop(0, rows, decode, 0)

    gather_tokens = (lax.div(iota((CHUNK, CHUNK * qlen), 1), qlen) == iota((CHUNK, CHUNK * qlen), 0)).astype(jnp.bfloat16)

    def back(offset):
        return pltpu.make_async_remote_copy(
            src_ref=scores_ref.at[offset],
            dst_ref=returned_ref.at[me],
            send_sem=back_send_sem.at[offset],
            recv_sem=back_recv_sem.at[me],
            device_id={AXIS: holder_of_mine(offset)},
            device_id_type=pl.DeviceIdType.MESH,
        )

    def send_back(offset, carry):
        back(offset).start()
        return carry

    def add_up(i):
        scored = split_dot(gather_tokens, maxima_ref[...], NT, True)
        for g in range(CHUNK):
            at = i * CHUNK + g
            scores_ref[lax.div(at, cap), pl.ds(lax.rem(at, cap), 1), pl.ds(0, rows)] = scored[g : g + 1, :]

    def chunk(i, carry):
        first = i * CHUNK
        lax.fori_loop(lax.div(first - 1 + cap, cap), lax.div(first + CHUNK - 1, cap) + 1, wait_query_if, 0)
        lax.fori_loop(jnp.maximum(done_before(i - 2), 1), jnp.maximum(done_before(i - 1), 1), send_back, 0)
        add_up(jnp.maximum(i - 1, 0))
        block = recv_ref[pl.ds(first, CHUNK)].reshape(CHUNK * qlen, dim)
        for r in range(rows):
            similar = dot(tokens_ref[r], block, NT)
            maxima_ref[r : r + 1, :] = jnp.max(similar, axis=0, keepdims=True)
        return carry

    def done_before(i):
        return lax.div(jnp.maximum(i, 0) * CHUNK, cap)

    def wait_query_if(offset, carry):
        @pl.when(offset >= 1)
        def _():
            outgoing(offset).wait_recv()

        return carry

    lax.fori_loop(0, steps, chunk, 0)
    add_up(steps - 1)

    def wait_sent(offset, carry):
        outgoing(offset).wait_send()
        return carry

    lax.fori_loop(1, n, wait_sent, 0)
    lax.fori_loop(max((steps - 2) * CHUNK // cap, 1), n, send_back, 0)
    returned_ref[me] = scores_ref[0]

    spread = (lax.div(iota((LANES, n * padded), 1), padded) == iota((LANES, n * padded), 0)).astype(jnp.bfloat16)
    wide_slot = dot(slot_of, spread, NN)
    wide_iota = iota((count, n * padded), 1)
    chosen = wide_slot == lax.rem(wide_iota, padded).astype(jnp.float32)
    picks = jnp.concatenate(
        [
            jnp.where(chosen & (lax.div(wide_iota, padded * per_group) == g), 1.0, 0.0).astype(jnp.bfloat16)
            for g in range(groups)
        ],
        axis=0,
    )

    def wait_back(offset, carry):
        peer = partner(offset)
        pltpu.make_async_remote_copy(
            src_ref=scores_ref.at[offset],
            dst_ref=returned_ref.at[peer],
            send_sem=back_send_sem.at[offset],
            recv_sem=back_recv_sem.at[peer],
            device_id={AXIS: peer},
            device_id_type=pl.DeviceIdType.MESH,
        ).wait_recv()
        return carry

    lax.fori_loop(1, n, wait_back, 0)
    placed = [pltpu.roll(returned_ref[k], k % per_group * rows, 1) for k in range(n)]
    values = split_dot(picks, jnp.concatenate(placed, axis=0), NN, True)
    result = jnp.zeros((count, slots), jnp.float32)
    for c in range(slots):
        kept = jnp.zeros((count, LANES), jnp.float32)
        for g in range(groups):
            kept = jnp.where(
                holder_iota + g * LANES == stored_cols[c], values[g * count : (g + 1) * count, :], kept
            )
        result = jnp.where(slot_iota == c, jnp.sum(kept, axis=1, keepdims=True), result)
    out_ref[...] = jnp.where(slot_iota < counted, result, 0.0)

    def wait_back_sent(offset, carry):
        back(offset).wait_send()
        return carry

    lax.fori_loop(1, n, wait_back_sent, 0)


def local(
    query_tokens,
    candidates,
    cand_count,
    placement_map,
    passage_base,
    residual_codes,
    passage_lengths,
    bucket_weights,
):
    n = lax.axis_size(AXIS)
    count, qlen, dim = query_tokens.shape
    slots = candidates.shape[1]
    rows, plen, _ = passage_base.shape
    cap = count * OWNERS_Q // n + 3
    padded = -(-cap // 8) * 8
    total = placement_map.shape[0]
    vmem = pl.BlockSpec(memory_space=pltpu.VMEM)
    hbm = pl.BlockSpec(memory_space=pltpu.HBM)
    return pl.pallas_call(
        functools.partial(kernel, n, cap),
        out_shape=jax.ShapeDtypeStruct((count, slots), jnp.float32),
        in_specs=[hbm] * 8,
        out_specs=vmem,
        scratch_shapes=[
            pltpu.SMEM((1, bucket_weights.shape[0]), jnp.float32),
            pltpu.SMEM((1, rows), jnp.int32),
            pltpu.VMEM((count, qlen, dim), jnp.bfloat16),
            pltpu.VMEM((slots, count), jnp.int32),
            pltpu.VMEM((1, count), jnp.int32),
            pltpu.VMEM((1, total), jnp.int32),
            pltpu.VMEM((rows, plen, dim), passage_base.dtype),
            pltpu.VMEM((rows, plen, dim), jnp.int32),
            pltpu.VMEM((rows, plen, dim), jnp.bfloat16),
            pltpu.VMEM((n * cap, qlen, dim), jnp.bfloat16),
            pltpu.VMEM((n * cap, qlen, dim), jnp.bfloat16),
            pltpu.VMEM((n, LANES), jnp.int32),
            pltpu.SMEM((n, LANES), jnp.int32),
            pltpu.VMEM((rows, CHUNK * qlen), jnp.float32),
            pltpu.VMEM((n, padded, LANES), jnp.float32),
            pltpu.VMEM((n, padded, LANES), jnp.float32),
            pltpu.SemaphoreType.DMA((8,)),
            pltpu.SemaphoreType.DMA,
            pltpu.SemaphoreType.DMA((n,)),
            pltpu.SemaphoreType.DMA((n,)),
            pltpu.SemaphoreType.DMA((n,)),
            pltpu.SemaphoreType.DMA((n,)),
        ],
        compiler_params=pltpu.CompilerParams(
            collective_id=0, has_side_effects=True, vmem_limit_bytes=60 * 1024 * 1024
        ),
        name="rerank",
    )(
        bucket_weights.reshape(1, -1),
        passage_lengths.reshape(1, -1),
        query_tokens,
        candidates.T,
        cand_count.reshape(1, -1),
        placement_map.reshape(1, -1),
        passage_base,
        residual_codes,
    )


def solution(mesh):
    split = P(("groups", "shard"))
    return jax.shard_map(
        local,
        mesh=mesh,
        in_specs=(
            P(("groups", "shard"), None, None),
            P(("groups", "shard"), None),
            split,
            P("groups"),
            P(("groups", "shard"), None, None),
            P(("groups", "shard"), None, None),
            split,
            P("groups"),
        ),
        out_specs=P(("groups", "shard"), None),
        check_vma=False,
    )
```

```python
import functools

import jax
import jax.numpy as jnp
from jax import lax
from jax.experimental import pallas as pl
from jax.experimental.pallas import tpu as pltpu
from jax.sharding import PartitionSpec as P

OWNERS_Q = 3
CHUNK = 8
LANES = 128
EPSILON = 1e-06
AXIS = "shard"

NT = (((1,), (1,)), ((), ()))
NN = (((1,), (0,)), ((), ()))


def dot(a, b, dims):
    return lax.dot_general(a, b, dims, preferred_element_type=jnp.float32)


def split_dot(a, b, dims, exact_left):
    full = b if exact_left else a
    high = full.astype(jnp.bfloat16)
    low = (full - high.astype(jnp.float32)).astype(jnp.bfloat16)
    if exact_left:
        return dot(a, high, dims) + dot(a, low, dims)
    return dot(high, b, dims) + dot(low, b, dims)


def iota(shape, axis):
    return lax.broadcasted_iota(jnp.int32, shape, axis)


def kernel(
    n,
    cap,
    cold,
    inner,
    weights_hbm,
    lengths_hbm,
    queries_hbm,
    candidates_hbm,
    count_hbm,
    placement_hbm,
    base_hbm,
    codes_hbm,
    out_ref,
    weights_ref,
    lengths_ref,
    queries_ref,
    candidates_ref,
    count_ref,
    placement_ref,
    base_ref,
    codes_ref,
    tokens_ref,
    send_ref,
    recv_ref,
    source_vmem,
    source_smem,
    maxima_ref,
    scores_ref,
    returned_ref,
    load_sem,
    source_sem,
    send_sem,
    recv_sem,
    back_send_sem,
    back_recv_sem,
    line_send_sem,
    line_recv_sem,
    block_send_sem,
    block_recv_sem,
    late_send_sem,
    late_recv_sem,
):
    me = lax.axis_index(AXIS)
    rows, plen, dim = base_ref.shape
    count, qlen, _ = queries_ref.shape
    slots = candidates_ref.shape[0]
    total = placement_ref.shape[1]
    padded = scores_ref.shape[1]
    per_group = LANES // rows
    groups = n // per_group
    hot = cap - cold
    outer = n // inner
    common = n * cold
    common_steps = common // CHUNK
    steps = n * cap // CHUNK
    early_steps = common_steps * 2 // 3
    my_outer, my_inner = lax.div(me, inner), lax.rem(me, inner)
    tile = padded // 2

    def shift(position):
        return jnp.where(position == 0, 0, lax.rem(position + n // 2 - 2 + n - 1, n - 1) + 1)

    def partner(position):
        return lax.rem(me + shift(position), n)

    def holder_of_mine(position):
        return lax.rem(me + n - shift(position), n)

    pairs = (
        (candidates_hbm, candidates_ref),
        (count_hbm, count_ref),
        (placement_hbm, placement_ref),
        (queries_hbm, queries_ref),
        (weights_hbm, weights_ref),
        (lengths_hbm, lengths_ref),
        (base_hbm, base_ref),
        (codes_hbm, codes_ref),
    )
    loads = [pltpu.make_async_copy(src, dst, load_sem.at[i]) for i, (src, dst) in enumerate(pairs)]
    for load in loads:
        load.start()

    barrier = pltpu.get_barrier_semaphore()

    def greet(offset, carry):
        pl.semaphore_signal(barrier, inc=1, device_id={AXIS: partner(offset)}, device_id_type=pl.DeviceIdType.MESH)
        return carry

    lax.fori_loop(1, n, greet, 0)

    for load in loads[:3]:
        load.wait()
    square = (iota((count, count), 0) == iota((count, count), 1)).astype(jnp.bfloat16)

    def upright(flat):
        return dot(square, flat.astype(jnp.float32).astype(jnp.bfloat16), NT).astype(jnp.int32)

    listed = candidates_ref[...]
    candidates = upright(lax.div(listed, 64)) * 64 + upright(lax.rem(listed, 64))
    counted = upright(jnp.broadcast_to(count_ref[...], (8, count)))[:, 0:1]
    placement = placement_ref[...].astype(jnp.float32)
    passage_iota = iota((count, total), 1)
    slot_iota = iota((count, slots), 1)
    holder_iota = iota((count, LANES), 1)
    stored_cols = []
    present = jnp.zeros((count, LANES), jnp.float32)
    for c in range(slots):
        hit = passage_iota == candidates[:, c : c + 1]
        found = jnp.sum(jnp.where(hit, placement, 0.0), axis=1, keepdims=True).astype(jnp.int32)
        stored_cols.append(found)
        holder = jnp.where(c < counted, lax.div(found, rows), -1)
        present = jnp.where(holder_iota == holder, 1.0, present)
    earlier = (iota((count, count), 1) < iota((count, count), 0)).astype(jnp.bfloat16)
    slot_of = dot(earlier, present.astype(jnp.bfloat16), NN)
    slot_of = jnp.where(present > 0.0, slot_of, -1.0).astype(jnp.bfloat16)
    eye = (iota((n, LANES), 0) == iota((n, LANES), 1)).astype(jnp.bfloat16)
    slot_by_holder = dot(eye, slot_of, NT)
    query_iota = iota((n, count), 1)
    lane_iota = iota((n, LANES), 1)
    source = jnp.zeros((n, LANES), jnp.int32)
    for s in range(cap):
        match = jnp.where(slot_by_holder == float(s), query_iota.astype(jnp.float32), 0.0)
        which = jnp.sum(match, axis=1, keepdims=True)
        if s >= cold:
            which = jnp.broadcast_to(jnp.sum(which, axis=0, keepdims=True), which.shape)
        source = jnp.where(lane_iota == s, which.astype(jnp.int32), source)
    source_vmem[...] = source

    maxima_ref[...] = jnp.zeros_like(maxima_ref)
    scores_ref[...] = jnp.zeros_like(scores_ref)

    to_scalar = pltpu.make_async_copy(source_vmem, source_smem, source_sem)
    to_scalar.start()
    loads[3].wait()
    to_scalar.wait()

    def query_for(holder, s):
        return queries_ref[jnp.minimum(jnp.maximum(source_smem[holder, s], 0), count - 1)]

    def pack(position, carry):
        holder = partner(position)
        for s in range(cold):
            send_ref[position * cold + s] = query_for(holder, s)
        return carry

    def outgoing(position):
        return pltpu.make_async_remote_copy(
            src_ref=send_ref.at[pl.ds(position * cold, cold)],
            dst_ref=recv_ref.at[pl.ds(position * cold, cold)],
            send_sem=send_sem.at[position],
            recv_sem=recv_sem.at[position],
            device_id={AXIS: partner(position)},
            device_id_type=pl.DeviceIdType.MESH,
        )

    def along_line(place, slot):
        rows_of = pl.ds(common + (my_inner * outer + slot) * hot, hot)
        return pltpu.make_async_remote_copy(
            src_ref=recv_ref.at[rows_of],
            dst_ref=recv_ref.at[rows_of],
            send_sem=line_send_sem.at[place],
            recv_sem=line_recv_sem.at[slot],
            device_id={AXIS: place * inner + my_inner},
            device_id_type=pl.DeviceIdType.MESH,
        )

    def inside_block(place, slot):
        rows_of = pl.ds(common + slot * outer * hot, outer * hot)
        return pltpu.make_async_remote_copy(
            src_ref=recv_ref.at[rows_of],
            dst_ref=recv_ref.at[rows_of],
            send_sem=block_send_sem.at[place],
            recv_sem=block_recv_sem.at[slot],
            device_id={AXIS: my_outer * inner + place},
            device_id_type=pl.DeviceIdType.MESH,
        )

    for s in range(hot):
        recv_ref[common + (my_inner * outer + my_outer) * hot + s] = query_for(me, cold + s)
    pack(1, 0)
    pl.semaphore_wait(barrier, n - 1)

    def start_line(k, carry):
        along_line(lax.rem(my_outer + k, outer), my_outer).start()
        return carry

    lax.fori_loop(1, outer, start_line, 0)

    def pack_and_send(position, carry):
        pack(position + 1, 0)
        outgoing(position).start()
        return carry

    lax.fori_loop(1, n - 1, pack_and_send, 0)
    for s in range(cold):
        recv_ref[s] = query_for(me, s)
    outgoing(n - 1).start()

    def pass_on():
        def wait_line(k, carry):
            along_line(my_outer, lax.rem(my_outer + k, outer)).wait_recv()
            return carry

        lax.fori_loop(1, outer, wait_line, 0)

        def start_block(k, carry):
            inside_block(lax.rem(my_inner + k, inner), my_inner).start()
            return carry

        lax.fori_loop(1, inner, start_block, 0)

    for load in loads[4:]:
        load.wait()
    token_iota = iota((plen, dim), 0)

    def decode(r, carry):
        codes = codes_ref[r]
        low = jnp.where(codes < 1, weights_ref[0, 0], weights_ref[0, 1])
        high = jnp.where(codes < 3, weights_ref[0, 2], weights_ref[0, 3])
        summed = base_ref[r].astype(jnp.float32) + jnp.where(codes < 2, low, high)
        inverse = lax.rsqrt(jnp.sum(summed * summed, axis=1, keepdims=True) + EPSILON)
        unit = summed * inverse
        unit = jnp.where(token_iota < lengths_ref[0, r], unit, unit[0:1, :])
        tokens_ref[r] = unit.astype(jnp.bfloat16)
        return carry

    lax.fori_loop(0, rows // 2, decode, 0)
    pass_on()
    lax.fori_loop(rows // 2, rows, decode, 0)

    gather_tokens = (lax.div(iota((CHUNK, CHUNK * qlen), 1), qlen) == iota((CHUNK, CHUNK * qlen), 0)).astype(jnp.bfloat16)

    def returning(position, owner, half, semaphores):
        return pltpu.make_async_remote_copy(
            src_ref=scores_ref.at[position, pl.ds(half * tile, tile)],
            dst_ref=returned_ref.at[owner, pl.ds(half * tile, tile)],
            send_sem=semaphores[0].at[position],
            recv_sem=semaphores[1].at[owner],
            device_id={AXIS: holder_of_mine(position)},
            device_id_type=pl.DeviceIdType.MESH,
        )

    early = (back_send_sem, back_recv_sem)
    late = (late_send_sem, late_recv_sem)

    def send_back(position, carry):
        returning(position, me, 0, early).start()
        return carry

    def send_late(position, carry):
        returning(position, me, 1, late).start()
        return carry

    def add_up():
        return split_dot(gather_tokens, maxima_ref[...], NT, True)

    def keep_common(scored, first):
        for g in range(CHUNK):
            at = first + g
            scores_ref[lax.div(at, cold), pl.ds(lax.rem(at, cold), 1), pl.ds(0, rows)] = scored[g : g + 1, :]

    def keep_hot(scored, first):
        for g in range(CHUNK):
            at = first - common + g
            place = lax.div(at, hot)
            sender = lax.rem(place, outer) * inner + lax.div(place, outer)
            away = lax.rem(me + n - sender, n)
            position = jnp.where(away == 0, 0, lax.rem(away - n // 2 + n - 1, n - 1) + 1)
            scores_ref[position, pl.ds(tile + lax.rem(at, hot), 1), pl.ds(0, rows)] = scored[g : g + 1, :]

    def match(first):
        block = recv_ref[pl.ds(first, CHUNK)].reshape(CHUNK * qlen, dim)
        for r in range(rows):
            similar = dot(tokens_ref[r], block, NT)
            maxima_ref[r : r + 1, :] = jnp.max(similar, axis=0, keepdims=True)

    def arrive(position, carry):
        @pl.when(position >= 1)
        def _():
            outgoing(position).wait_recv()

        return carry

    def done_before(i):
        return lax.div(jnp.maximum(i, 0) * CHUNK, cold)

    def common_chunk(i, carry):
        first = i * CHUNK
        lax.fori_loop(lax.div(first - 1 + cold, cold), lax.div(first + CHUNK - 1, cold) + 1, arrive, 0)
        lax.fori_loop(jnp.maximum(done_before(i - 2), 1), jnp.maximum(done_before(i - 1), 1), send_back, 0)
        if carry is None:
            keep_hot(add_up(), n * cap - CHUNK)
        else:
            keep_common(add_up(), jnp.maximum(i - 1, 0) * CHUNK)
        match(first)
        return carry

    def hot_chunk(i, carry):
        keep_hot(add_up(), common + jnp.maximum(i - 1, 0) * CHUNK)
        match(common + i * CHUNK)
        return carry

    lax.fori_loop(0, early_steps, common_chunk, 0)
    keep_common(add_up(), (early_steps - 1) * CHUNK)

    def wait_block(k, carry):
        inside_block(my_inner, lax.rem(my_inner + k, inner)).wait_recv()
        return carry

    lax.fori_loop(1, inner, wait_block, 0)
    lax.fori_loop(0, steps - common_steps, hot_chunk, 0)
    common_chunk(early_steps, None)
    lax.fori_loop(1, n, send_late, 0)
    lax.fori_loop(early_steps + 1, common_steps, common_chunk, 0)
    keep_common(add_up(), common - CHUNK)

    def wait_sent(offset, carry):
        outgoing(offset).wait_send()
        return carry

    lax.fori_loop(1, n, wait_sent, 0)
    lax.fori_loop(max((common_steps - 2) * CHUNK // cold, 1), n, send_back, 0)

    def line_sent(k, carry):
        along_line(lax.rem(my_outer + k, outer), my_outer).wait_send()
        return carry

    lax.fori_loop(1, outer, line_sent, 0)

    def block_sent(k, carry):
        inside_block(lax.rem(my_inner + k, inner), my_inner).wait_send()
        return carry

    lax.fori_loop(1, inner, block_sent, 0)
    returned_ref[me] = scores_ref[0]

    spread = (lax.div(iota((LANES, n * padded), 1), padded) == iota((LANES, n * padded), 0)).astype(jnp.bfloat16)
    wide_slot = dot(slot_of, spread, NN)
    wide_iota = iota((count, n * padded), 1)
    wide_place = lax.rem(wide_iota, padded)
    wide_place = jnp.where(
        wide_place < tile,
        jnp.where(wide_place < cold, wide_place, -2),
        jnp.where(wide_place < tile + hot, wide_place - tile + cold, -2),
    )
    chosen = wide_slot == wide_place.astype(jnp.float32)
    picks = jnp.concatenate(
        [
            jnp.where(chosen & (lax.div(wide_iota, padded * per_group) == g), 1.0, 0.0).astype(jnp.bfloat16)
            for g in range(groups)
        ],
        axis=0,
    )

    def wait_back(position, carry):
        owner = holder_of_mine(position)
        returning(position, owner, 0, early).wait_recv()
        returning(position, owner, 1, late).wait_recv()
        return carry

    lax.fori_loop(1, n, wait_back, 0)
    placed = [pltpu.roll(returned_ref[k], k % per_group * rows, 1) for k in range(n)]
    values = split_dot(picks, jnp.concatenate(placed, axis=0), NN, True)
    result = jnp.zeros((count, slots), jnp.float32)
    for c in range(slots):
        kept = jnp.zeros((count, LANES), jnp.float32)
        for g in range(groups):
            kept = jnp.where(
                holder_iota + g * LANES == stored_cols[c], values[g * count : (g + 1) * count, :], kept
            )
        result = jnp.where(slot_iota == c, jnp.sum(kept, axis=1, keepdims=True), result)
    out_ref[...] = jnp.where(slot_iota < counted, result, 0.0)

    def wait_back_sent(offset, carry):
        returning(offset, me, 0, early).wait_send()
        returning(offset, me, 1, late).wait_send()
        return carry

    lax.fori_loop(1, n, wait_back_sent, 0)


def local(
    query_tokens,
    candidates,
    cand_count,
    placement_map,
    passage_base,
    residual_codes,
    passage_lengths,
    bucket_weights,
):
    n = lax.axis_size(AXIS)
    count, qlen, dim = query_tokens.shape
    slots = candidates.shape[1]
    rows, plen, _ = passage_base.shape
    cap = count * OWNERS_Q // n + 3
    cold = -(-count * OWNERS_Q // n)
    padded = 2 * (-(-max(cold, cap - cold) // 8) * 8)
    inner = 1 << ((n.bit_length() - 1) // 2)
    total = placement_map.shape[0]
    vmem = pl.BlockSpec(memory_space=pltpu.VMEM)
    hbm = pl.BlockSpec(memory_space=pltpu.HBM)
    return pl.pallas_call(
        functools.partial(kernel, n, cap, cold, inner),
        out_shape=jax.ShapeDtypeStruct((count, slots), jnp.float32),
        in_specs=[hbm] * 8,
        out_specs=vmem,
        scratch_shapes=[
            pltpu.SMEM((1, bucket_weights.shape[0]), jnp.float32),
            pltpu.SMEM((1, rows), jnp.int32),
            pltpu.VMEM((count, qlen, dim), jnp.bfloat16),
            pltpu.VMEM((slots, count), jnp.int32),
            pltpu.VMEM((1, count), jnp.int32),
            pltpu.VMEM((1, total), jnp.int32),
            pltpu.VMEM((rows, plen, dim), passage_base.dtype),
            pltpu.VMEM((rows, plen, dim), jnp.int32),
            pltpu.VMEM((rows, plen, dim), jnp.bfloat16),
            pltpu.VMEM((n * cold, qlen, dim), jnp.bfloat16),
            pltpu.VMEM((n * cap, qlen, dim), jnp.bfloat16),
            pltpu.VMEM((n, LANES), jnp.int32),
            pltpu.SMEM((n, LANES), jnp.int32),
            pltpu.VMEM((rows, CHUNK * qlen), jnp.float32),
            pltpu.VMEM((n, padded, LANES), jnp.float32),
            pltpu.VMEM((n, padded, LANES), jnp.float32),
            pltpu.SemaphoreType.DMA((8,)),
            pltpu.SemaphoreType.DMA,
            pltpu.SemaphoreType.DMA((n,)),
            pltpu.SemaphoreType.DMA((n,)),
            pltpu.SemaphoreType.DMA((n,)),
            pltpu.SemaphoreType.DMA((n,)),
            pltpu.SemaphoreType.DMA((n // inner,)),
            pltpu.SemaphoreType.DMA((n // inner,)),
            pltpu.SemaphoreType.DMA((inner,)),
            pltpu.SemaphoreType.DMA((inner,)),
            pltpu.SemaphoreType.DMA((n,)),
            pltpu.SemaphoreType.DMA((n,)),
        ],
        compiler_params=pltpu.CompilerParams(
            collective_id=0, has_side_effects=True, vmem_limit_bytes=60 * 1024 * 1024
        ),
        name="rerank",
    )(
        bucket_weights.reshape(1, -1),
        passage_lengths.reshape(1, -1),
        query_tokens,
        candidates.T,
        cand_count.reshape(1, -1),
        placement_map.reshape(1, -1),
        passage_base,
        residual_codes,
    )


def solution(mesh):
    split = P(("groups", "shard"))
    return jax.shard_map(
        local,
        mesh=mesh,
        in_specs=(
            P(("groups", "shard"), None, None),
            P(("groups", "shard"), None),
            split,
            P("groups"),
            P(("groups", "shard"), None, None),
            P(("groups", "shard"), None, None),
            split,
            P("groups"),
        ),
        out_specs=P(("groups", "shard"), None),
        check_vma=False,
    )
```

```python
import functools

import jax
import jax.numpy as jnp
from jax import lax
from jax.experimental import pallas as pl
from jax.experimental.pallas import tpu as pltpu
from jax.sharding import PartitionSpec as P

OWNERS_Q = 3
CHUNK = 16
LANES = 128
EPSILON = 1e-06
AXIS = "shard"

NT = (((1,), (1,)), ((), ()))
NN = (((1,), (0,)), ((), ()))


def dot(a, b, dims):
    return lax.dot_general(a, b, dims, preferred_element_type=jnp.float32)


def split_dot(a, b, dims, exact_left):
    full = b if exact_left else a
    high = full.astype(jnp.bfloat16)
    low = (full - high.astype(jnp.float32)).astype(jnp.bfloat16)
    if exact_left:
        return dot(a, high, dims) + dot(a, low, dims)
    return dot(high, b, dims) + dot(low, b, dims)


def iota(shape, axis):
    return lax.broadcasted_iota(jnp.int32, shape, axis)


def kernel(
    n,
    cap,
    cold,
    inner,
    weights_hbm,
    lengths_hbm,
    queries_hbm,
    candidates_hbm,
    count_hbm,
    placement_hbm,
    base_hbm,
    codes_hbm,
    out_ref,
    weights_ref,
    lengths_ref,
    queries_ref,
    candidates_ref,
    count_ref,
    placement_ref,
    base_ref,
    codes_ref,
    tokens_ref,
    send_ref,
    recv_ref,
    source_vmem,
    source_smem,
    maxima_ref,
    scores_ref,
    returned_ref,
    load_sem,
    source_sem,
    send_sem,
    recv_sem,
    back_send_sem,
    back_recv_sem,
    line_send_sem,
    line_recv_sem,
    block_send_sem,
    block_recv_sem,
    late_send_sem,
    late_recv_sem,
):
    me = lax.axis_index(AXIS)
    rows, plen, dim = base_ref.shape
    count, qlen, _ = queries_ref.shape
    slots = candidates_ref.shape[0]
    total = placement_ref.shape[1]
    padded = scores_ref.shape[1]
    per_group = LANES // rows
    groups = n // per_group
    hot = cap - cold
    outer = n // inner
    common = n * cold
    common_steps = common // CHUNK
    steps = n * cap // CHUNK
    early_steps = common_steps // 3
    my_outer, my_inner = lax.div(me, inner), lax.rem(me, inner)
    tile = padded // 2

    def shift(position):
        return position

    def partner(position):
        return lax.rem(me + shift(position), n)

    def holder_of_mine(position):
        return lax.rem(me + n - shift(position), n)

    pairs = (
        (candidates_hbm, candidates_ref),
        (count_hbm, count_ref),
        (placement_hbm, placement_ref),
        (queries_hbm, queries_ref),
        (weights_hbm, weights_ref),
        (lengths_hbm, lengths_ref),
        (base_hbm, base_ref),
        (codes_hbm, codes_ref),
    )
    loads = [pltpu.make_async_copy(src, dst, load_sem.at[i]) for i, (src, dst) in enumerate(pairs)]
    for load in loads:
        load.start()

    barrier = pltpu.get_barrier_semaphore()

    def greet(offset, carry):
        pl.semaphore_signal(barrier, inc=1, device_id={AXIS: partner(offset)}, device_id_type=pl.DeviceIdType.MESH)
        return carry

    lax.fori_loop(1, n, greet, 0)

    for load in loads[:3]:
        load.wait()
    square = (iota((count, count), 0) == iota((count, count), 1)).astype(jnp.bfloat16)

    def upright(flat):
        return dot(square, flat.astype(jnp.float32).astype(jnp.bfloat16), NT).astype(jnp.int32)

    listed = candidates_ref[...]
    candidates = upright(lax.div(listed, 64)) * 64 + upright(lax.rem(listed, 64))
    counted = upright(jnp.broadcast_to(count_ref[...], (8, count)))[:, 0:1]
    placement = placement_ref[...].astype(jnp.float32)
    passage_iota = iota((count, total), 1)
    slot_iota = iota((count, slots), 1)
    holder_iota = iota((count, LANES), 1)
    stored_cols = []
    present = jnp.zeros((count, LANES), jnp.float32)
    for c in range(slots):
        hit = passage_iota == candidates[:, c : c + 1]
        found = jnp.sum(jnp.where(hit, placement, 0.0), axis=1, keepdims=True).astype(jnp.int32)
        stored_cols.append(found)
        holder = jnp.where(c < counted, lax.div(found, rows), -1)
        present = jnp.where(holder_iota == holder, 1.0, present)
    earlier = (iota((count, count), 1) < iota((count, count), 0)).astype(jnp.bfloat16)
    slot_of = dot(earlier, present.astype(jnp.bfloat16), NN)
    slot_of = jnp.where(present > 0.0, slot_of, -1.0).astype(jnp.bfloat16)
    eye = (iota((n, LANES), 0) == iota((n, LANES), 1)).astype(jnp.bfloat16)
    slot_by_holder = dot(eye, slot_of, NT)
    query_iota = iota((n, count), 1)
    lane_iota = iota((n, LANES), 1)
    source = jnp.zeros((n, LANES), jnp.int32)
    for s in range(cap):
        match = jnp.where(slot_by_holder == float(s), query_iota.astype(jnp.float32), 0.0)
        which = jnp.sum(match, axis=1, keepdims=True)
        if s >= cold:
            which = jnp.broadcast_to(jnp.sum(which, axis=0, keepdims=True), which.shape)
        source = jnp.where(lane_iota == s, which.astype(jnp.int32), source)
    source_vmem[...] = source

    maxima_ref[...] = jnp.zeros_like(maxima_ref)
    scores_ref[...] = jnp.zeros_like(scores_ref)

    to_scalar = pltpu.make_async_copy(source_vmem, source_smem, source_sem)
    to_scalar.start()
    loads[3].wait()
    to_scalar.wait()

    def query_for(holder, s):
        return queries_ref[jnp.minimum(jnp.maximum(source_smem[holder, s], 0), count - 1)]

    def pack(position, carry):
        holder = partner(position)
        for s in range(cold):
            send_ref[position * cold + s] = query_for(holder, s)
        return carry

    def outgoing(position):
        return pltpu.make_async_remote_copy(
            src_ref=send_ref.at[pl.ds(position * cold, cold)],
            dst_ref=recv_ref.at[pl.ds(position * cold, cold)],
            send_sem=send_sem.at[position],
            recv_sem=recv_sem.at[position],
            device_id={AXIS: partner(position)},
            device_id_type=pl.DeviceIdType.MESH,
        )

    def along_line(place, slot):
        rows_of = pl.ds(common + (my_inner * outer + slot) * hot, hot)
        return pltpu.make_async_remote_copy(
            src_ref=recv_ref.at[rows_of],
            dst_ref=recv_ref.at[rows_of],
            send_sem=line_send_sem.at[place],
            recv_sem=line_recv_sem.at[slot],
            device_id={AXIS: place * inner + my_inner},
            device_id_type=pl.DeviceIdType.MESH,
        )

    def inside_block(place, slot):
        rows_of = pl.ds(common + slot * outer * hot, outer * hot)
        return pltpu.make_async_remote_copy(
            src_ref=recv_ref.at[rows_of],
            dst_ref=recv_ref.at[rows_of],
            send_sem=block_send_sem.at[place],
            recv_sem=block_recv_sem.at[slot],
            device_id={AXIS: my_outer * inner + place},
            device_id_type=pl.DeviceIdType.MESH,
        )

    for s in range(hot):
        recv_ref[common + (my_inner * outer + my_outer) * hot + s] = query_for(me, cold + s)
    pack(1, 0)
    pl.semaphore_wait(barrier, n - 1)

    def start_line(k, carry):
        along_line(lax.rem(my_outer + k, outer), my_outer).start()
        return carry

    lax.fori_loop(1, outer, start_line, 0)

    def pack_and_send(position, carry):
        pack(position + 1, 0)
        outgoing(position).start()
        return carry

    lax.fori_loop(1, n - 1, pack_and_send, 0)
    for s in range(cold):
        recv_ref[s] = query_for(me, s)
    outgoing(n - 1).start()

    def pass_on():
        def wait_line(k, carry):
            along_line(my_outer, lax.rem(my_outer + k, outer)).wait_recv()
            return carry

        lax.fori_loop(1, outer, wait_line, 0)

        def start_block(k, carry):
            inside_block(lax.rem(my_inner + k, inner), my_inner).start()
            return carry

        lax.fori_loop(1, inner, start_block, 0)

    for load in loads[4:]:
        load.wait()
    token_iota = iota((plen, dim), 0)

    def decode(r, carry):
        codes = codes_ref[r]
        low = jnp.where(codes < 1, weights_ref[0, 0], weights_ref[0, 1])
        high = jnp.where(codes < 3, weights_ref[0, 2], weights_ref[0, 3])
        summed = base_ref[r].astype(jnp.float32) + jnp.where(codes < 2, low, high)
        inverse = lax.rsqrt(jnp.sum(summed * summed, axis=1, keepdims=True) + EPSILON)
        unit = summed * inverse
        unit = jnp.where(token_iota < lengths_ref[0, r], unit, unit[0:1, :])
        tokens_ref[r] = unit.astype(jnp.bfloat16)
        return carry

    lax.fori_loop(0, rows // 2, decode, 0, unroll=2)
    pass_on()
    lax.fori_loop(rows // 2, rows, decode, 0, unroll=2)

    gather_tokens = (lax.div(iota((CHUNK, CHUNK * qlen), 1), qlen) == iota((CHUNK, CHUNK * qlen), 0)).astype(jnp.bfloat16)

    def returning(position, owner, half, semaphores):
        return pltpu.make_async_remote_copy(
            src_ref=scores_ref.at[position, pl.ds(half * tile, tile)],
            dst_ref=returned_ref.at[owner, pl.ds(half * tile, tile)],
            send_sem=semaphores[0].at[position],
            recv_sem=semaphores[1].at[owner],
            device_id={AXIS: holder_of_mine(position)},
            device_id_type=pl.DeviceIdType.MESH,
        )

    early = (back_send_sem, back_recv_sem)
    late = (late_send_sem, late_recv_sem)

    def send_back(position, carry):
        returning(position, me, 0, early).start()
        return carry

    def send_late(position, carry):
        returning(position, me, 1, late).start()
        return carry

    def add_up():
        return split_dot(gather_tokens, maxima_ref[...], NT, True)

    def walk(first, size):
        whole = lax.div(first, size)
        rest = first - whole * size
        for g in range(CHUNK):
            yield g, whole, rest
            full = rest + 1 == size
            whole = jnp.where(full, whole + 1, whole)
            rest = jnp.where(full, 0, rest + 1)

    def keep_common(scored, first):
        for g, position, slot in walk(first, cold):
            scores_ref[position, pl.ds(slot, 1), pl.ds(0, rows)] = scored[g : g + 1, :]

    def keep_hot(scored, first):
        for g, place, slot in walk(first - common, hot):
            sender = lax.rem(place, outer) * inner + lax.div(place, outer)
            position = jnp.where(sender > me, me + n - sender, me - sender)
            scores_ref[position, pl.ds(tile + slot, 1), pl.ds(0, rows)] = scored[g : g + 1, :]

    def match(first):
        block = recv_ref[pl.ds(first, CHUNK)].reshape(CHUNK * qlen, dim)
        for r in range(rows):
            similar = dot(tokens_ref[r], block, NT)
            maxima_ref[r : r + 1, :] = jnp.max(similar, axis=0, keepdims=True)

    def arrive(position, carry):
        @pl.when(position >= 1)
        def _():
            outgoing(position).wait_recv()

        return carry

    def done_before(i):
        return lax.div(jnp.maximum(i, 0) * CHUNK, cold)

    def common_chunk(i, carry):
        first = i * CHUNK
        lax.fori_loop(lax.div(first - 1 + cold, cold), lax.div(first + CHUNK - 1, cold) + 1, arrive, 0)
        lax.fori_loop(jnp.maximum(done_before(i - 2), 1), jnp.maximum(done_before(i - 1), 1), send_back, 0)
        if carry is None:
            keep_hot(add_up(), n * cap - CHUNK)
        else:
            keep_common(add_up(), jnp.maximum(i - 1, 0) * CHUNK)
        match(first)
        return carry

    def hot_chunk(i, carry):
        keep_hot(add_up(), common + jnp.maximum(i - 1, 0) * CHUNK)
        match(common + i * CHUNK)
        return carry

    lax.fori_loop(0, early_steps, common_chunk, 0)
    keep_common(add_up(), (early_steps - 1) * CHUNK)

    def wait_block(k, carry):
        inside_block(my_inner, lax.rem(my_inner + k, inner)).wait_recv()
        return carry

    lax.fori_loop(1, inner, wait_block, 0)
    lax.fori_loop(0, steps - common_steps, hot_chunk, 0)
    common_chunk(early_steps, None)
    lax.fori_loop(1, n, send_late, 0)
    lax.fori_loop(early_steps + 1, common_steps, common_chunk, 0)
    keep_common(add_up(), common - CHUNK)

    def wait_sent(offset, carry):
        outgoing(offset).wait_send()
        return carry

    lax.fori_loop(1, n, wait_sent, 0)
    lax.fori_loop(max((common_steps - 2) * CHUNK // cold, 1), n, send_back, 0)

    def line_sent(k, carry):
        along_line(lax.rem(my_outer + k, outer), my_outer).wait_send()
        return carry

    lax.fori_loop(1, outer, line_sent, 0)

    def block_sent(k, carry):
        inside_block(lax.rem(my_inner + k, inner), my_inner).wait_send()
        return carry

    lax.fori_loop(1, inner, block_sent, 0)
    returned_ref[me] = scores_ref[0]

    spread = (lax.div(iota((LANES, n * padded), 1), padded) == iota((LANES, n * padded), 0)).astype(jnp.bfloat16)
    wide_slot = dot(slot_of, spread, NN)
    wide_iota = iota((count, n * padded), 1)
    wide_place = lax.rem(wide_iota, padded)
    wide_place = jnp.where(
        wide_place < tile,
        jnp.where(wide_place < cold, wide_place, -2),
        jnp.where(wide_place < tile + hot, wide_place - tile + cold, -2),
    )
    chosen = wide_slot == wide_place.astype(jnp.float32)
    picks = jnp.concatenate(
        [
            jnp.where(chosen & (lax.div(wide_iota, padded * per_group) == g), 1.0, 0.0).astype(jnp.bfloat16)
            for g in range(groups)
        ],
        axis=0,
    )

    def wait_back(position, carry):
        owner = holder_of_mine(position)
        returning(position, owner, 0, early).wait_recv()
        returning(position, owner, 1, late).wait_recv()
        return carry

    lax.fori_loop(1, n, wait_back, 0)
    placed = [pltpu.roll(returned_ref[k], k % per_group * rows, 1) for k in range(n)]
    values = split_dot(picks, jnp.concatenate(placed, axis=0), NN, True)
    result = jnp.zeros((count, slots), jnp.float32)
    for c in range(slots):
        kept = jnp.zeros((count, LANES), jnp.float32)
        for g in range(groups):
            kept = jnp.where(
                holder_iota + g * LANES == stored_cols[c], values[g * count : (g + 1) * count, :], kept
            )
        result = jnp.where(slot_iota == c, jnp.sum(kept, axis=1, keepdims=True), result)
    out_ref[...] = jnp.where(slot_iota < counted, result, 0.0)

    def wait_back_sent(offset, carry):
        returning(offset, me, 0, early).wait_send()
        returning(offset, me, 1, late).wait_send()
        return carry

    lax.fori_loop(1, n, wait_back_sent, 0)


def local(
    query_tokens,
    candidates,
    cand_count,
    placement_map,
    passage_base,
    residual_codes,
    passage_lengths,
    bucket_weights,
):
    n = lax.axis_size(AXIS)
    count, qlen, dim = query_tokens.shape
    slots = candidates.shape[1]
    rows, plen, _ = passage_base.shape
    cap = count * OWNERS_Q // n + 3
    cold = -(-count * OWNERS_Q // n)
    padded = 2 * (-(-max(cold, cap - cold) // 8) * 8)
    inner = 1 << ((n.bit_length() - 1) // 2)
    total = placement_map.shape[0]
    vmem = pl.BlockSpec(memory_space=pltpu.VMEM)
    hbm = pl.BlockSpec(memory_space=pltpu.HBM)
    return pl.pallas_call(
        functools.partial(kernel, n, cap, cold, inner),
        out_shape=jax.ShapeDtypeStruct((count, slots), jnp.float32),
        in_specs=[hbm] * 8,
        out_specs=vmem,
        scratch_shapes=[
            pltpu.SMEM((1, bucket_weights.shape[0]), jnp.float32),
            pltpu.SMEM((1, rows), jnp.int32),
            pltpu.VMEM((count, qlen, dim), jnp.bfloat16),
            pltpu.VMEM((slots, count), jnp.int32),
            pltpu.VMEM((1, count), jnp.int32),
            pltpu.VMEM((1, total), jnp.int32),
            pltpu.VMEM((rows, plen, dim), passage_base.dtype),
            pltpu.VMEM((rows, plen, dim), jnp.int32),
            pltpu.VMEM((rows, plen, dim), jnp.bfloat16),
            pltpu.VMEM((n * cold, qlen, dim), jnp.bfloat16),
            pltpu.VMEM((n * cap, qlen, dim), jnp.bfloat16),
            pltpu.VMEM((n, LANES), jnp.int32),
            pltpu.SMEM((n, LANES), jnp.int32),
            pltpu.VMEM((rows, CHUNK * qlen), jnp.float32),
            pltpu.VMEM((n, padded, LANES), jnp.float32),
            pltpu.VMEM((n, padded, LANES), jnp.float32),
            pltpu.SemaphoreType.DMA((8,)),
            pltpu.SemaphoreType.DMA,
            pltpu.SemaphoreType.DMA((n,)),
            pltpu.SemaphoreType.DMA((n,)),
            pltpu.SemaphoreType.DMA((n,)),
            pltpu.SemaphoreType.DMA((n,)),
            pltpu.SemaphoreType.DMA((n // inner,)),
            pltpu.SemaphoreType.DMA((n // inner,)),
            pltpu.SemaphoreType.DMA((inner,)),
            pltpu.SemaphoreType.DMA((inner,)),
            pltpu.SemaphoreType.DMA((n,)),
            pltpu.SemaphoreType.DMA((n,)),
        ],
        compiler_params=pltpu.CompilerParams(
            collective_id=0, has_side_effects=True, vmem_limit_bytes=60 * 1024 * 1024
        ),
        name="rerank",
    )(
        bucket_weights.reshape(1, -1),
        passage_lengths.reshape(1, -1),
        query_tokens,
        candidates.T,
        cand_count.reshape(1, -1),
        placement_map.reshape(1, -1),
        passage_base,
        residual_codes,
    )


def solution(mesh):
    split = P(("groups", "shard"))
    return jax.shard_map(
        local,
        mesh=mesh,
        in_specs=(
            P(("groups", "shard"), None, None),
            P(("groups", "shard"), None),
            split,
            P("groups"),
            P(("groups", "shard"), None, None),
            P(("groups", "shard"), None, None),
            split,
            P("groups"),
        ),
        out_specs=P(("groups", "shard"), None),
        check_vma=False,
    )
```
